32 devices in a mesh: views: 4 (over z), bricks: 8 (over y, x, core).
Axes of the slice: x: 2, y: 2, z: 4, core: 2. Of those that a mesh axis runs over, the one named last changes fastest.
Arguments:
- tile_pixel: int32 [4, 8, 32], P('views', 'bricks'), may hold values from 0 to 15
- tile_voxel: int32 [4, 8, 32], P('views', 'bricks'), may hold values from 0 to 63
- tile_count: int32 [4, 8], P('views', 'bricks'), may hold values from 8 to 32, as said below
- features: bfloat16 [4, 8, 16, 64, 128], P('views', 'bricks'), may hold values from -6 to 6
- interp: bfloat16 [4, 8, 32, 128, 512], P('views', 'bricks'), may hold values from -0.5 to 0.5
- conv_weight: bfloat16 [3, 3, 3, 64, 64], replicated, may hold values from -0.15625 to 0.15625
- conv_bias: float32 [64], replicated, may hold values from -3 to 3
- smooth_coef: float32 [64, 128, 128], P('bricks', 'views'), may hold values from 0.04 to 0.16
Outputs:
- volume: bfloat16 [64, 64, 128, 128], P(None, 'bricks', 'views')
The draws below stay inside these ranges and needn't reach their ends.
Inputs may be any that keep to these rules, and one draw needn't show every extreme that they name: `tile_count`: between 8 and 32 live tiles a device; counts are shared largely within a view group; some device has all 32 slots live in every draw.
All inputs are finite; a program needn't handle non-finite values.
Results may differ from the reference program's by a relative error of at most 0.0037.
Values may be sent and summed in bfloat16 or wider, within the bound.
A program may use at most 256 MiB of HBM per device.

```python
import math
import jax
import jax.numpy as jnp
from jax import lax

C = 64
PIX = 128
Z = 128
BX = 8
BY = 32
PIXB = 16
BLK_DEV = 64
VOXB = 512
X = 64
Y = 128
N_VIEWS = 4
N_BRICKS = 8
DEVICES = 32


def draw_tile_count(key, part):
    key_top = jax.random.fold_in(key, 11)
    key_drop = jax.random.fold_in(key, 12)
    key_pick = jax.random.fold_in(key, 13)
    lowest = DEVICES // 4
    view_top = jax.random.randint(key_top, (N_VIEWS, 1), lowest, DEVICES + 1)
    dropped = jax.random.randint(key_drop, (N_VIEWS, N_BRICKS), 0, DEVICES // 4 + 1)
    counts = jnp.maximum(view_top - dropped, lowest).reshape(-1)
    picked = jax.random.randint(key_pick, (), 0, N_VIEWS * N_BRICKS)
    counts = jnp.where(jnp.arange(N_VIEWS * N_BRICKS) == picked, DEVICES, counts)
    return counts.reshape(N_VIEWS, N_BRICKS).astype(jnp.int32)


def with_ends(array, rng, smallest, top_value):
    dims = array.shape
    spot = [jax.random.randint(jax.random.fold_in(rng, axis), (), 0, dims[axis]) for axis in range(len(dims))]
    array = array.at[tuple(spot)].set(smallest)
    longest = dims.index(max(dims))
    spot[longest] = (spot[longest] + 1) % dims[longest]
    return array.at[tuple(spot)].set(top_value)


def levels(rng, shape, cuts, low, top_value):
    gain, own = 1.0, jax.random.fold_in(rng, 6)
    for axis_at, shards_of in cuts:
        draws = jnp.exp(jax.random.uniform(jax.random.fold_in(own, axis_at), (shards_of,), jnp.float32, low / len(cuts), top_value / len(cuts)))
        gain = gain * jnp.repeat(draws, shape[axis_at] // shards_of).reshape([-1 if axis == axis_at else 1 for axis in range(len(shape))])
    return gain


def scatter_about(stream_key, dims, scale, most, cuts=(), kind=jnp.bfloat16):
    gain = levels(stream_key, dims, cuts, -0.22, 0.18) if cuts else 1.0
    values = jax.random.normal(stream_key, dims, jnp.float32) * scale * gain
    return jnp.minimum(jnp.maximum(values, -most), most).astype(kind)


def setup_inputs(seed: int = 0) -> dict:
    seeds = jax.random.split(jax.random.key(seed), 9)
    return {
        "tile_pixel": with_ends(jax.random.randint(seeds[0], (N_VIEWS, N_BRICKS, N_VIEWS * N_BRICKS), 0, PIXB), jax.random.fold_in(seeds[0], 1), 0, PIXB - 1).astype(jnp.int32),
        "tile_voxel": with_ends(jax.random.randint(seeds[1], (N_VIEWS, N_BRICKS, N_VIEWS * N_BRICKS), 0, BLK_DEV), jax.random.fold_in(seeds[1], 1), 0, BLK_DEV - 1).astype(jnp.int32),
        "tile_count": draw_tile_count(jax.random.fold_in(seeds[8], 71), 0),
        "features": scatter_about(seeds[3], (N_VIEWS, N_BRICKS, PIXB, C, PIX), 1.0, 6.0, ((0, 4), (1, 8))),
        "interp": scatter_about(seeds[4], (N_VIEWS, N_BRICKS, N_VIEWS * N_BRICKS, PIX, VOXB), PIX ** -0.5, 0.5, ((0, 4), (1, 8))),
        "conv_weight": scatter_about(seeds[5], (3, 3, 3, C, C), (27 * C) ** -0.5, 0.15625),
        "conv_bias": scatter_about(seeds[6], (C,), 0.5, 3.0, (), jnp.float32),
        "smooth_coef": jnp.clip(jnp.exp(math.log(0.16) - 1.3862944 * jax.random.uniform(seeds[7], (X, Y, Z), jnp.float32) ** levels(seeds[7], (X, Y, Z), ((0, 8), (1, 4)), -0.2, 0.2)), 0.04, 0.16),
    }


def lift_step(total, item):
    feats, tiles, pixel_ids, voxel_ids, count, sender = item
    slot_ids = jnp.arange(DEVICES, dtype=jnp.int32)
    offset = jnp.remainder(sender * 37, DEVICES)
    live = (jnp.remainder(slot_ids - offset, DEVICES) < count).astype(jnp.float32)
    chosen = feats[pixel_ids]
    part = jnp.einsum("dcp,dpv->dcv", chosen.astype(jnp.float32), tiles.astype(jnp.float32))
    rounded = lax.optimization_barrier(part.astype(jnp.bfloat16))
    part = rounded.astype(jnp.float32)
    total = total.at[slot_ids, voxel_ids].add(part * live[:, None, None])
    return total, None


def convolve_slab(stacked, weights, conv_bias, width_x, width_y):
    total = jnp.zeros((C, width_x, width_y, Z), jnp.float32)
    for shift_x in range(3):
        for shift_y in range(3):
            window = stacked[:, shift_x:shift_x + width_x, shift_y:shift_y + width_y, :]
            total = total + jnp.einsum("oi,ixyz->oxyz", weights[shift_x * 3 + shift_y].astype(jnp.float32), window.astype(jnp.float32))
    return jax.nn.relu(total + conv_bias[:, None, None, None])


def reference(tile_pixel, tile_voxel, tile_count, features, interp, conv_weight, conv_bias, smooth_coef):
    senders = jnp.arange(DEVICES, dtype=jnp.int32)
    items = (features.reshape(DEVICES, PIXB, C, PIX), interp.reshape(DEVICES, DEVICES, PIX, VOXB),
             tile_pixel.reshape(DEVICES, DEVICES), tile_voxel.reshape(DEVICES, DEVICES),
             tile_count.reshape(DEVICES), senders)
    start = jnp.zeros((DEVICES, BLK_DEV, C, VOXB), jnp.float32)
    blocks, unused = lax.scan(lift_step, start, items)
    blocks = blocks.reshape(N_VIEWS, N_BRICKS, BX, BY // 4, C, 4, Z)
    lifted = jnp.transpose(blocks, (4, 1, 2, 0, 3, 5, 6)).reshape(C, X, Y, Z)
    rectified = jax.nn.relu(lifted).astype(jnp.bfloat16)
    padded = jnp.pad(rectified, ((0, 0), (1, 1), (1, 1), (1, 1)))
    stacked = jnp.concatenate([padded[..., 0:Z], padded[..., 1:Z + 1], padded[..., 2:Z + 2]], axis=0)
    weights = jnp.transpose(conv_weight, (0, 1, 3, 2, 4)).reshape(9, C, 3 * C)

    def slab(index):
        piece = lax.dynamic_slice_in_dim(stacked, index * BX, BX + 2, 1)
        return convolve_slab(piece, weights, conv_bias, BX, Y)

    slabs = lax.map(slab, jnp.arange(N_BRICKS, dtype=jnp.int32))
    gated = jnp.transpose(slabs, (1, 0, 2, 3, 4)).reshape(C, X, Y, Z)
    beside_all = jnp.pad(gated, ((0, 0), (1, 1), (1, 1), (1, 1)))
    beside = beside_all[:, 2:, 1:-1, 1:-1] + beside_all[:, :-2, 1:-1, 1:-1]
    beside = beside + beside_all[:, 1:-1, 2:, 1:-1] + beside_all[:, 1:-1, :-2, 1:-1]
    beside = beside + beside_all[:, 1:-1, 1:-1, 2:] + beside_all[:, 1:-1, 1:-1, :-2]
    volume = gated + smooth_coef[None] * (beside - 6.0 * gated)
    return volume.astype(jnp.bfloat16)
```

```python
import functools

import jax
import jax.numpy as jnp
from jax import lax
from jax.experimental import pallas as pl
from jax.experimental.pallas import tpu as pltpu
from jax.sharding import PartitionSpec as P

MESH = pl.DeviceIdType.MESH
DIRS = ((0, 1), (0, -1), (1, 0), (-1, 0), (1, 1), (1, -1), (-1, 1), (-1, -1))
SENDS = (
    (0, 1, 0), (0, -1, 0), (1, 0, None), (-1, 0, None),
    (1, 1, None), (1, -1, None), (-1, 1, None), (-1, -1, None),
    (0, 1, 1), (0, -1, 1),
)
GROUP = 4
LIMIT = 60 * 1024 * 1024


def exchange_kernel(
    views, bricks, pixel_ref, voxel_ref, count_ref, feats_ref, tiles_ref, out_ref,
    tiles, part, got, sums, mark, marks, table, index,
    tile_sem, send_sem, recv_sem, mark_send, mark_recv, table_sem,
):
    v = lax.axis_index("views")
    b = lax.axis_index("bricks")
    slots = tiles.shape[0]
    me = v * bricks + b
    parts, _, ch, depth = part.shape
    size_x, size_y = out_ref.shape[:2]
    across = size_y // parts
    blocks = size_x * across
    order = [parts - 1] + list(range(parts - 1))

    def peer(k):
        turn = k + (views // 2) * bricks
        return lax.rem(v + turn // bricks, views), lax.rem(b + lax.rem(turn, bricks), bricks)

    def place(k):
        pv, pb = peer(k)
        return pv * bricks + pb

    def loop(low, high, body, unroll=1):
        def step(i, _):
            body(i)
            return 0

        lax.fori_loop(low, high, step, 0, unroll=unroll)

    own = (views - views // 2) * bricks % slots

    def fetch(k):
        slot = place(k)
        return pltpu.make_async_copy(tiles_ref.at[slot], tiles.at[slot], tile_sem.at[slot])

    loop(0, slots, lambda k: fetch(k).start())
    barrier = pltpu.get_barrier_semaphore()

    def greet(k):
        @pl.when(k != own)
        def _():
            pl.semaphore_signal(barrier, inc=1, device_id=peer(k), device_id_type=MESH)

    loop(0, slots, greet)

    offset = lax.rem(me * 37, slots)

    def note(s):
        turn = lax.rem(s - offset + slots, slots)
        ident = jnp.where(turn < count_ref[0, 0], voxel_ref[0, 0, s], blocks)
        mark[s] = jnp.full(mark.shape[1:], ident, jnp.int32)

    loop(0, slots, note)

    def send_mark(k):
        return pltpu.make_async_remote_copy(
            src_ref=mark.at[place(k)], dst_ref=marks.at[me],
            send_sem=mark_send, recv_sem=mark_recv,
            device_id=peer(k), device_id_type=MESH,
        )

    def send_part(q, k):
        return pltpu.make_async_remote_copy(
            src_ref=part.at[q, place(k)], dst_ref=got.at[q, me],
            send_sem=send_sem.at[q], recv_sem=recv_sem.at[q],
            device_id=peer(k), device_id_type=MESH,
        )

    def push(q, k):
        @pl.when(k != own)
        def _():
            send_part(q, k).start()

        @pl.when(k == own)
        def _():
            pltpu.make_async_copy(part.at[q, me], got.at[q, me], recv_sem.at[q]).start()

    def lift(k):
        slot = place(k)
        fetch(k).wait()
        value = jnp.dot(
            feats_ref[pixel_ref[0, 0, slot]], tiles[slot], preferred_element_type=jnp.float32
        ).astype(jnp.bfloat16)
        for q in range(parts):
            part[q, slot] = value[:, q * depth : (q + 1) * depth]

    lift(0)
    pl.semaphore_wait(barrier, slots - 1)

    def greet_mark(k):
        @pl.when(k != own)
        def _():
            send_mark(k).start()

        @pl.when(k == own)
        def _():
            pltpu.make_async_copy(mark.at[me], marks.at[me], mark_recv).start()

    loop(0, slots, greet_mark)

    def lift_push(k):
        lift(k)
        push(order[0], k - 1)

    loop(1, slots, lift_push)
    push(order[0], slots - 1)
    for q in order[1:]:
        loop(0, slots, lambda k, q=q: push(q, k))

    pltpu.make_async_copy(marks, marks, mark_recv).wait()
    lane = lax.broadcasted_iota(jnp.int32, marks.shape[1:], 1)
    row = jnp.full(lane.shape, -1, jnp.int32)
    row = lax.fori_loop(0, slots, lambda d, r: jnp.where(lane == d, marks[d], r), row)

    def newest(match):
        found = jnp.max(jnp.where(match, lane, -1), axis=1, keepdims=True)
        return jnp.where(found < 0, slots, found)

    table[0] = lax.fori_loop(
        0, slots,
        lambda d, t: jnp.where(lane == d, newest((row == marks[d]) & (lane < d)), t),
        jnp.zeros(lane.shape, jnp.int32),
    )
    table[1] = lax.fori_loop(
        0, blocks,
        lambda i, t: jnp.where(lane == i, newest(row == i), t),
        jnp.zeros(lane.shape, jnp.int32),
    )
    to_scalar = pltpu.make_async_copy(table, index, table_sem)
    to_scalar.start()
    to_scalar.wait()
    sums[slots] = jnp.zeros(sums.shape[1:], jnp.float32)

    for q in order:
        pltpu.make_async_copy(got.at[q], got.at[q], recv_sem.at[q]).wait()

        def add(d, q=q):
            sums[d] = sums[index[0, 0, d]] + got[q, d].astype(jnp.float32)

        def put(i, q=q):
            value = jnp.maximum(sums[index[1, 0, i]], 0.0).astype(jnp.bfloat16)
            out_ref[i // across, lax.rem(i, across) * parts + q] = value

        loop(0, slots, add, 4)
        loop(0, blocks, put, 4)

    for q in range(parts):
        sent = part.at[q, pl.ds(0, slots - 1)]
        pltpu.make_async_copy(sent, sent, send_sem.at[q]).wait()
    sent = mark.at[pl.ds(0, slots - 1)]
    pltpu.make_async_copy(sent, sent, mark_send).wait()


def exchange(pixel, voxel, count, feats, tiles, size_x, size_y, depth, views, bricks):
    slots, pixels, voxels = tiles.shape
    ch = feats.shape[1]
    parts = voxels // depth
    smem = pl.BlockSpec(memory_space=pltpu.SMEM)
    vmem = pl.BlockSpec(memory_space=pltpu.VMEM)
    anyspec = pl.BlockSpec(memory_space=pl.ANY)
    return pl.pallas_call(
        functools.partial(exchange_kernel, views, bricks),
        out_shape=jax.ShapeDtypeStruct((size_x, size_y, ch, depth), jnp.bfloat16),
        in_specs=[smem, smem, smem, vmem, anyspec],
        out_specs=vmem,
        scratch_shapes=[
            pltpu.VMEM(tiles.shape, jnp.bfloat16),
            pltpu.VMEM((parts, slots, ch, depth), jnp.bfloat16),
            pltpu.VMEM((parts, slots, ch, depth), jnp.bfloat16),
            pltpu.VMEM((slots + 1, ch, depth), jnp.float32),
            pltpu.VMEM((slots, 8, 128), jnp.int32),
            pltpu.VMEM((slots, 8, 128), jnp.int32),
            pltpu.VMEM((2, 8, 128), jnp.int32),
            pltpu.SMEM((2, 8, 128), jnp.int32),
            pltpu.SemaphoreType.DMA((slots,)),
            pltpu.SemaphoreType.DMA((parts,)),
            pltpu.SemaphoreType.DMA((parts,)),
            pltpu.SemaphoreType.DMA,
            pltpu.SemaphoreType.DMA,
            pltpu.SemaphoreType.DMA,
        ],
        compiler_params=pltpu.CompilerParams(
            collective_id=1, has_side_effects=True, vmem_limit_bytes=LIMIT
        ),
        name="exchange",
    )(pixel, voxel, count, feats, tiles)


def conv_kernel(
    views, bricks, r_ref, w_ref, bias_ref, coef_ref, out_ref,
    padded, prod, gated, obuf, own_sem, send_sem, recv_sem, out_sem,
):
    v = lax.axis_index("views")
    b = lax.axis_index("bricks")
    size_x, size_y, ch, depth = r_ref.shape
    wide = 3 * ch

    def there(dv, db):
        return (v + dv >= 0) & (v + dv < views) & (b + db >= 0) & (b + db < bricks)

    def count(dv, db):
        return jnp.where(there(dv, db), 1, 0)

    own = pltpu.make_async_copy(
        r_ref, padded.at[pl.ds(2, size_x), pl.ds(2, size_y)], own_sem
    )
    own.start()

    barrier = pltpu.get_barrier_semaphore()
    total = 0
    for dv, db in DIRS:
        total = total + count(dv, db)

        @pl.when(there(dv, db))
        def _(dv=dv, db=db):
            pl.semaphore_signal(barrier, inc=1, device_id=(v + dv, b + db), device_id_type=MESH)

    pl.semaphore_wait(barrier, total)

    def span(delta, size, plane=None):
        if delta == 0:
            return pl.ds(0, size), pl.ds(2, size)
        if plane is None:
            low, width = 0, 2
        else:
            low, width = (1 - plane if delta == 1 else plane), 1
        if delta == 1:
            return pl.ds(size - 2 + low, width), pl.ds(low, width)
        return pl.ds(low, width), pl.ds(size + 2 + low, width)

    def copy(k):
        dv, db, plane = SENDS[k]
        from_x, to_x = span(db, size_x, plane)
        from_y, to_y = span(dv, size_y)
        return pltpu.make_async_remote_copy(
            src_ref=r_ref.at[from_x, from_y],
            dst_ref=padded.at[to_x, to_y],
            send_sem=send_sem.at[k],
            recv_sem=recv_sem.at[k],
            device_id=(v + dv, b + db),
            device_id_type=MESH,
        )

    for k, (dv, db, _) in enumerate(SENDS):

        @pl.when(there(dv, db))
        def _(k=k):
            copy(k).start()

    def receive(k):
        dv, db, plane = SENDS[k]
        _, to_x = span(db, size_x, plane)
        _, to_y = span(dv, size_y)

        @pl.when(there(-dv, -db))
        def _():
            copy(k).wait_recv()

        @pl.when(jnp.logical_not(there(-dv, -db)))
        def _():
            view = padded.at[to_x, to_y]
            view[...] = jnp.zeros(view.shape, jnp.bfloat16)

    lane = lax.broadcasted_iota(jnp.int32, (ch, depth), 1)

    def beside_z(low, high):
        before = jnp.where(lane == 0, 0.0, pltpu.roll(low, 1, 1))
        after = jnp.where(lane == depth - 1, 0.0, pltpu.roll(high, depth - 1, 1))
        return before + after

    def start_rows(slot, g, y):
        tall = [
            jnp.concatenate([padded[g + dx, y + dy + j] for j in range(GROUP)], axis=1)
            for dx in range(3)
            for dy in range(3)
        ]
        prod[slot] = jnp.dot(
            w_ref[...], jnp.concatenate(tall, axis=0), preferred_element_type=jnp.float32
        )

    def finish_rows(slot, g, y):
        x_all = b * size_x + g - 1
        x_fits = (x_all >= 0) & (x_all < bricks * size_x)
        for j in range(GROUP):
            at = slice(j * depth, (j + 1) * depth)
            value = prod[slot, ch : 2 * ch, at]
            value = value + beside_z(prod[slot, 0:ch, at], prod[slot, 2 * ch : wide, at])
            value = jnp.maximum(value + bias_ref[...], 0.0)
            y_all = v * size_y + y + j - 1
            fits = x_fits & (y_all >= 0) & (y_all < views * size_y)
            gated[g, y + j] = value * jnp.where(fits, 1.0, 0.0)

    def loop(low, high, body, unroll=1):
        def step(i, _):
            body(i)
            return 0

        lax.fori_loop(low, high, step, 0, unroll=unroll)

    groups = size_y // GROUP

    def smooth_rows(x, y):
        here = gated[x + 1, y + 1]
        beside = gated[x, y + 1] + gated[x + 2, y + 1] + gated[x + 1, y] + gated[x + 1, y + 2]
        beside = beside + beside_z(here, here)
        coef = coef_ref[x, pl.ds(y, 1), :]
        obuf[x, y] = (here + coef * (beside - 6.0 * here)).astype(jnp.bfloat16)

    def put(x):
        pltpu.make_async_copy(obuf.at[x], out_ref.at[x], out_sem.at[x]).start()

    def run_rows(g, starts, x=None):
        for i, y in enumerate(starts):
            start_rows(i % 2, g, y)
            if x is not None:
                for j in range(GROUP):
                    if i * GROUP + j < size_y:
                        smooth_rows(x, i * GROUP + j)
            if i:
                finish_rows((i - 1) % 2, g, starts[i - 1])
        finish_rows((len(starts) - 1) % 2, g, starts[-1])
        if x is not None:
            put(x)

    def loop(low, high, body):
        def step(i, _):
            body(i)
            return 0

        lax.fori_loop(low, high, step, 0)

    middle = [GROUP * c for c in range(1, size_y // GROUP)]
    ends = [0, size_y + 2 - GROUP]
    rows = [0] + middle + [size_y + 2 - GROUP]

    own.wait()
    loop(2, 5, lambda g: run_rows(g, middle))
    receive(2)
    receive(3)
    loop(2, 5, lambda g: run_rows(g, ends))
    loop(5, size_x, lambda g: run_rows(g, rows, g - 3))
    low_first = b < bricks // 2

    def boundary(i):
        low_side = (i < 2) == low_first
        odd = lax.rem(i, 2)
        for db, side in ((1, low_side), (-1, jnp.logical_not(low_side))):
            for plane in range(2):
                keys = [
                    k
                    for k, (dv, step, part) in enumerate(SENDS)
                    if step == db and (part == plane or (part is None and plane == 0))
                ]

                @pl.when(side & (odd == plane))
                def _(keys=keys):
                    for k in keys:
                        receive(k)

        g = jnp.where(low_side, 1 - odd, size_x + odd)
        ahead = jnp.where(i == 1, 1, jnp.where(i == 2, 0, size_x - 2))
        behind = jnp.where(i == 1, size_x - 2, jnp.where(i == 2, size_x - 1, 1))
        x = jnp.where(i == 0, size_x - 3, jnp.where(low_first, ahead, behind))
        run_rows(g, rows, x)

    loop(0, 4, boundary)
    last = jnp.where(low_first, size_x - 1, 0)

    def finish(y):
        for j in range(GROUP):
            smooth_rows(last, y * GROUP + j)

    loop(0, size_y // GROUP, finish)
    put(last)
    for x in range(size_x):
        pltpu.make_async_copy(obuf.at[x], out_ref.at[x], out_sem.at[x]).wait()
    for k, (dv, db, _) in enumerate(SENDS):

        @pl.when(there(dv, db))
        def _(k=k):
            copy(k).wait_send()


def convolve_smooth(rect, weights, bias, coef, views, bricks):
    size_x, size_y, ch, depth = rect.shape
    vmem = pl.BlockSpec(memory_space=pltpu.VMEM)
    anyspec = pl.BlockSpec(memory_space=pl.ANY)
    return pl.pallas_call(
        functools.partial(conv_kernel, views, bricks),
        out_shape=jax.ShapeDtypeStruct(rect.shape, jnp.bfloat16),
        in_specs=[anyspec, vmem, vmem, vmem],
        out_specs=anyspec,
        scratch_shapes=[
            pltpu.VMEM((size_x + 4, size_y + 4, ch, depth), jnp.bfloat16),
            pltpu.VMEM((2, 3 * ch, GROUP * depth), jnp.float32),
            pltpu.VMEM((size_x + 2, size_y + 2, ch, depth), jnp.float32),
            pltpu.VMEM((size_x, size_y, ch, depth), jnp.bfloat16),
            pltpu.SemaphoreType.DMA,
            pltpu.SemaphoreType.DMA((len(SENDS),)),
            pltpu.SemaphoreType.DMA((len(SENDS),)),
            pltpu.SemaphoreType.DMA((size_x,)),
        ],
        compiler_params=pltpu.CompilerParams(
            collective_id=0, has_side_effects=True, vmem_limit_bytes=LIMIT
        ),
        name="conv",
    )(rect, weights, bias, coef)


def on_device(
    views, bricks,
    tile_pixel, tile_voxel, tile_count, features, interp, conv_weight, conv_bias, smooth_coef
):
    feats = features[0, 0]
    tiles = interp[0, 0]
    channels = feats.shape[1]
    size_x, size_y, depth = smooth_coef.shape
    rect = exchange(
        tile_pixel, tile_voxel, tile_count, feats, tiles, size_x, size_y, depth, views, bricks
    )
    weights = jnp.transpose(conv_weight, (2, 3, 0, 1, 4)).reshape(3 * channels, 9 * channels)
    bias = jnp.broadcast_to(conv_bias[:, None], (channels, depth))
    out = convolve_smooth(rect, weights, bias, smooth_coef, views, bricks)
    return jnp.transpose(out, (2, 0, 1, 3))


def solution(mesh):
    in_specs = (
        P("views", "bricks", None),
        P("views", "bricks", None),
        P("views", "bricks"),
        P("views", "bricks", None, None, None),
        P("views", "bricks", None, None, None),
        P(),
        P(),
        P("bricks", "views", None),
    )
    out_specs = P(None, "bricks", "views", None)
    body = functools.partial(on_device, mesh.shape["views"], mesh.shape["bricks"])
    return jax.shard_map(body, mesh=mesh, in_specs=in_specs, out_specs=out_specs, check_vma=False)
```

```python
import functools

import jax
import jax.numpy as jnp
from jax import lax
from jax.experimental import pallas as pl
from jax.experimental.pallas import tpu as pltpu
from jax.sharding import PartitionSpec as P

MESH = pl.DeviceIdType.MESH
GROUP = 4
RING = 32
LIMIT = 60 * 1024 * 1024
PAIRS = ((0, 1), (1, 2), (0, 2))


def lift_conv_kernel(
    views, bricks, pixel_ref, voxel_ref, count_ref, feats_ref, tiles_ref, w_ref, bias_ref,
    coef_ref, out_ref,
    tiles, part, got, sums, mark, marks, table, index, pad, acc, prod, obuf, pair, one, shift,
    tile_sem, send_sem, recv_sem, mark_send, mark_recv, table_sem, halo_send, halo_recv, out_sem,
):
    v = lax.axis_index("views")
    b = lax.axis_index("bricks")
    slots = voxel_ref.shape[2]
    ring = tiles.shape[0]
    me = v * bricks + b
    parts, _, ch, depth = part.shape
    size_x, size_y = obuf.shape[:2]
    across = size_y // parts
    blocks = size_x * across
    order = [parts - 1] + list(range(parts - 1))
    wide = 3 * ch

    def loop(low, high, body, unroll=1):
        def step(i, _):
            body(i)
            return 0

        lax.fori_loop(low, high, step, 0, unroll=unroll)

    def peer(k):
        turn = k + (views // 2) * bricks
        return lax.rem(v + turn // bricks, views), lax.rem(b + lax.rem(turn, bricks), bricks)

    def place(k):
        pv, pb = peer(k)
        return pv * bricks + pb

    own = (views - views // 2) * bricks % slots

    def fetch(k):
        slot = lax.rem(k, ring)
        return pltpu.make_async_copy(tiles_ref.at[place(k)], tiles.at[slot], tile_sem.at[slot])

    loop(0, ring, lambda k: fetch(k).start())
    barrier = pltpu.get_barrier_semaphore()

    def greet(k):
        @pl.when(k != own)
        def _():
            pl.semaphore_signal(barrier, inc=1, device_id=peer(k), device_id_type=MESH)

    loop(0, slots, greet)
    offset = lax.rem(me * 37, slots)

    def note(s):
        turn = lax.rem(s - offset + slots, slots)
        ident = jnp.where(turn < count_ref[0, 0], voxel_ref[0, 0, s], blocks)
        mark[s] = jnp.full(mark.shape[1:], ident, jnp.int32)

    loop(0, slots, note)

    def push(q, k):
        @pl.when(k != own)
        def _():
            pltpu.make_async_remote_copy(
                src_ref=part.at[q, place(k)], dst_ref=got.at[q, me],
                send_sem=send_sem.at[q], recv_sem=recv_sem.at[q],
                device_id=peer(k), device_id_type=MESH,
            ).start()

        @pl.when(k == own)
        def _():
            pltpu.make_async_copy(part.at[q, me], got.at[q, me], recv_sem.at[q]).start()

    def push_mark(k):
        @pl.when(k != own)
        def _():
            pltpu.make_async_remote_copy(
                src_ref=mark.at[place(k)], dst_ref=marks.at[me],
                send_sem=mark_send, recv_sem=mark_recv,
                device_id=peer(k), device_id_type=MESH,
            ).start()

        @pl.when(k == own)
        def _():
            pltpu.make_async_copy(mark.at[me], marks.at[me], mark_recv).start()

    def lift(k):
        slot = place(k)
        fetch(k).wait()
        value = jnp.dot(
            feats_ref[pixel_ref[0, 0, slot]], tiles[lax.rem(k, ring)],
            preferred_element_type=jnp.float32,
        ).astype(jnp.bfloat16)
        for q in range(parts):
            part[q, slot] = value[:, q * depth : (q + 1) * depth]
        if ring < slots:

            @pl.when(k + ring < slots)
            def _():
                fetch(k + ring).start()

    def lift_push(k):
        lift(k)
        push(order[0], k - 1)

    lift(0)
    pl.semaphore_wait(barrier, slots - 1)
    loop(1, slots, lift_push)
    push(order[0], slots - 1)
    loop(0, slots, push_mark)
    for q in order[1:]:
        loop(0, slots, lambda k, q=q: push(q, k))

    def there(dv, db):
        return (v + dv >= 0) & (v + dv < views) & (b + db >= 0) & (b + db < bricks)

    def low_row(q):
        return 1 if 2 * q >= parts else 0

    def edges(q):
        dv = 1 if 2 * q >= parts else -1
        return ((0, 1), (0, -1), (dv, 0), (dv, 1), (dv, -1))

    def span(q, dv, db):
        width = 2 if dv == 0 or q in (0, parts - 1) else 1
        if db == 0:
            from_x, to_x = pl.ds(2, size_x), pl.ds(2, size_x)
        elif db == 1:
            from_x, to_x = pl.ds(size_x + 2 - width, width), pl.ds(2 - width, width)
        else:
            from_x, to_x = pl.ds(2, width), pl.ds(size_x + 2, width)
        if dv == 0:
            return from_x, pl.ds(low_row(q), across), to_x, pl.ds(low_row(q), across)
        if dv == 1:
            return from_x, pl.ds(across, 1), to_x, pl.ds(0, 1)
        return from_x, pl.ds(0, 1), to_x, pl.ds(across, 1)

    def halo(q, k):
        dv, db = edges(q)[k]
        from_x, from_y, to_x, to_y = span(q, dv, db)
        return pltpu.make_async_remote_copy(
            src_ref=pad.at[q, from_x, from_y], dst_ref=pad.at[q, to_x, to_y],
            send_sem=halo_send.at[q, k], recv_sem=halo_recv.at[q, k],
            device_id=(v + dv, b + db), device_id_type=MESH,
        )

    for q in range(parts):
        for k, (dv, db) in enumerate(edges(q)):

            @pl.when(jnp.logical_not(there(-dv, -db)))
            def _(q=q, dv=dv, db=db):
                _, _, to_x, to_y = span(q, dv, db)
                view = pad.at[q, to_x, to_y]
                view[...] = jnp.zeros(view.shape, jnp.bfloat16)

    for dy in range(3):
        one[dy] = jnp.concatenate(
            [
                jnp.concatenate([w_ref[dx, dy, dz] for dz in range(3)], axis=0)
                for dx in range(3)
            ],
            axis=1,
        )
    for i, (first, second) in enumerate(PAIRS):
        pair[i] = jnp.concatenate([one[first], one[second]], axis=1)
    tall = lax.broadcasted_iota(jnp.int32, (ch, ch), 0)
    flat = lax.broadcasted_iota(jnp.int32, (ch, ch), 1)
    spread = jnp.where(tall == flat, jnp.broadcast_to(bias_ref[...], (ch, ch)), 0.0)
    shift[...] = jnp.broadcast_to(jnp.sum(spread, axis=1, keepdims=True), shift.shape)

    pltpu.make_async_copy(marks, marks, mark_recv).wait()
    lane = lax.broadcasted_iota(jnp.int32, marks.shape[1:], 1)
    row = jnp.full(lane.shape, -1, jnp.int32)
    row = lax.fori_loop(0, slots, lambda d, r: jnp.where(lane == d, marks[d], r), row)

    def newest(match):
        found = jnp.max(jnp.where(match, lane, -1), axis=1, keepdims=True)
        return jnp.where(found < 0, slots, found)

    table[0] = lax.fori_loop(
        0, slots,
        lambda d, t: jnp.where(lane == d, newest((row == marks[d]) & (lane < d)), t),
        jnp.zeros(lane.shape, jnp.int32),
    )
    table[1] = lax.fori_loop(
        0, blocks,
        lambda i, t: jnp.where(lane == i, newest(row == i), t),
        jnp.zeros(lane.shape, jnp.int32),
    )
    to_scalar = pltpu.make_async_copy(table, index, table_sem)
    to_scalar.start()
    to_scalar.wait()
    sums[slots] = jnp.zeros(sums.shape[1:], jnp.float32)

    def receive(q):
        pltpu.make_async_copy(got.at[q], got.at[q], recv_sem.at[q]).wait()

        def add(d):
            sums[d] = sums[index[0, 0, d]] + got[q, d].astype(jnp.float32)

        def put(i):
            i = lax.rem(i + (size_x - 2) * across, blocks)
            value = jnp.maximum(sums[index[1, 0, i]], 0.0).astype(jnp.bfloat16)
            pad[q, 2 + i // across, lax.rem(i, across) + low_row(q)] = value

        loop(0, slots, add, 4)
        loop(0, blocks, put, 4)
        for k, (dv, db) in enumerate(edges(q)):

            @pl.when(there(dv, db))
            def _(k=k):
                halo(q, k).start()

    def halos(q):
        for k, (dv, db) in enumerate(edges(q)):

            @pl.when(there(-dv, -db))
            def _(k=k):
                halo(q, k).wait_recv()

    wave = lax.broadcasted_iota(jnp.int32, (ch, depth), 1)

    def beside_z(low, high):
        before = jnp.where(wave == 0, 0.0, pltpu.roll(low, 1, 1))
        after = jnp.where(wave == depth - 1, 0.0, pltpu.roll(high, depth - 1, 1))
        return before + after

    def start(slot, job):
        items, q, sources, weight, first, final = job
        n = len(items) * depth
        tall = [
            jnp.concatenate([pad[p, g + dx, y + dy] for g, y in items], axis=1)
            for p, dy in sources
            for dx in range(3)
        ]
        prod[slot, :, 0:n] = jnp.dot(
            weight[...], jnp.concatenate(tall, axis=0), preferred_element_type=jnp.float32
        )

    def finish(slot, job, keep=None):
        items, q, sources, weight, first, final = job
        for j, (g, y) in enumerate(items):
            at = slice(j * depth, (j + 1) * depth)
            value = prod[slot, ch : 2 * ch, at]
            value = value + beside_z(prod[slot, 0:ch, at], prod[slot, 2 * ch : wide, at])
            if not first:
                value = value + acc[g, q, y]
            if final:
                value = jnp.maximum(value + shift[...], 0.0)
                if keep is not None:
                    value = value * keep
            acc[g, q, y] = value

    def place_of(y):
        q = y % parts
        return q, y // parts + low_row(q)

    def smooth(x, y):
        here = acc[(x + 1,) + place_of(y)]
        beside = acc[(x,) + place_of(y)] + acc[(x + 2,) + place_of(y)]
        beside = beside + acc[(x + 1,) + place_of(y - 1)] + acc[(x + 1,) + place_of(y + 1)]
        beside = beside + beside_z(here, here)
        coef = coef_ref[x, y : y + 1, :]
        obuf[x, y] = (here + coef * (beside - 6.0 * here)).astype(jnp.bfloat16)

    def put_out(x):
        pltpu.make_async_copy(obuf.at[x], out_ref.at[x], out_sem.at[x]).start()

    def run(jobs, x=None, rows=(), keep=None):
        each = -(-len(rows) // len(jobs))
        for i, job in enumerate(jobs):
            start(i % 2, job)
            for y in rows[i * each : (i + 1) * each]:
                smooth(x, y)
            if i:
                finish((i - 1) % 2, jobs[i - 1], keep)
        finish((len(jobs) - 1) % 2, jobs[-1], keep)

    def plane(g, q, sources, weight, first, final):
        low = low_row(q)
        ys = [low + i for i in range(across)]
        return [
            ([(g, y) for y in ys[i : i + GROUP]], q, sources, weight, first, final)
            for i in range(0, across, GROUP)
        ]

    def line(y, q, sources, weight, first, final):
        gs = [1 + i for i in range(size_x)]
        return [
            ([(g, y) for g in gs[i : i + GROUP]], q, sources, weight, first, final)
            for i in range(0, size_x, GROUP)
        ]

    last = parts - 1
    both = ((last, 0), (0, 0))

    def wipe(gs, qs, ys):
        for g in gs:
            for q in qs:
                for y in ys:
                    acc[g, q, y] = jnp.zeros((ch, depth), jnp.float32)

    receive(order[0])
    receive(order[1])
    halos(order[0])
    halos(order[1])
    loop(
        0, size_x + 2,
        lambda g: run(
            plane(g, 0, both, pair.at[0], True, False)
            + plane(g, last, both, pair.at[1], True, False)
        ),
    )
    run(
        line(across, 0, both, pair.at[0], True, False)
        + line(0, last, both, pair.at[1], True, False)
    )
    receive(order[2])
    halos(order[2])
    loop(
        0, size_x + 2,
        lambda g: run(
            plane(g, 0, ((1, 0),), one.at[2], False, True)
            + plane(g, 1, ((0, 0), (1, 0)), pair.at[0], True, False)
            + plane(g, 2, ((1, -1), (last, 0)), pair.at[2], True, False)
        ),
    )
    run(line(across, 0, ((1, 0),), one.at[2], False, True))

    @pl.when(v == views - 1)
    def _():
        wipe(range(1, size_x + 1), (0,), (across,))

    @pl.when(b == 0)
    def _():
        wipe((0,), (0,), range(across))

    @pl.when(b == bricks - 1)
    def _():
        wipe((size_x + 1,), (0,), range(across))

    receive(order[3])

    def close(g):
        return (
            plane(g, 1, ((2, 1),), one.at[2], False, True)
            + plane(g, 2, ((2, 0),), one.at[1], False, True)
            + plane(g, last, ((2, 0),), one.at[0], False, True)
        )

    inner = list(range(1, size_y))
    whole = list(range(size_y))
    loop(2, 5, lambda g: run(close(g)))
    loop(5, size_x, lambda g: run(close(g), g - 3, inner))
    halos(order[3])
    run(line(0, last, ((2, 0),), one.at[0], False, True))

    @pl.when(v == 0)
    def _():
        wipe(range(1, size_x + 1), (last,), (0,))

    def early(x):
        smooth(x, 0)
        put_out(x)

    loop(2, size_x - 3, early)

    def rest(i):
        low = lax.rem(i, 2) == 0
        g = jnp.where(low, 1 - i // 2, size_x + i // 2)
        x = jnp.where(
            i == 0, size_x - 3, jnp.where(i == 1, 1, jnp.where(i == 2, size_x - 2, 0))
        )
        fits = jnp.where(i < 2, 0, jnp.where(low, b, bricks - 1 - b) - 1) >= 0
        run(close(g), x, whole, jnp.where(fits, 1.0, 0.0))
        put_out(x)

    loop(0, 4, rest)

    def ending(i):
        for j in range(parts):
            smooth_last(i, j)

    def smooth_last(k, q):
        x = size_x - 1
        base = k + low_row(q)

        def spot(p):
            if p < 0:
                return parts - 1, k + low_row(parts - 1) - 1
            if p >= parts:
                return 0, k + 1 + low_row(0)
            return p, k + low_row(p)

        here = acc[x + 1, q, base]
        beside = acc[x, q, base] + acc[x + 2, q, base]
        beside = beside + acc[(x + 1,) + spot(q - 1)] + acc[(x + 1,) + spot(q + 1)]
        beside = beside + beside_z(here, here)
        coef = coef_ref[x, pl.ds(k * parts + q, 1), :]
        value = here + coef * (beside - 6.0 * here)
        obuf[x, k * parts + q] = value.astype(jnp.bfloat16)

    loop(0, across, ending)
    put_out(size_x - 1)
    for x in range(size_x):
        pltpu.make_async_copy(obuf.at[x], out_ref.at[x], out_sem.at[x]).wait()
    for q in range(parts):
        sent = part.at[q, pl.ds(0, slots - 1)]
        pltpu.make_async_copy(sent, sent, send_sem.at[q]).wait()
        for k, (dv, db) in enumerate(edges(q)):

            @pl.when(there(dv, db))
            def _(q=q, k=k):
                halo(q, k).wait_send()

    sent = mark.at[pl.ds(0, slots - 1)]
    pltpu.make_async_copy(sent, sent, mark_send).wait()


def lift_conv(pixel, voxel, count, feats, tiles, weight, bias, coef, views, bricks):
    slots, pixels, voxels = tiles.shape
    ch = feats.shape[1]
    size_x, size_y, depth = coef.shape
    parts = voxels // depth
    across = size_y // parts
    assert parts == 4
    smem = pl.BlockSpec(memory_space=pltpu.SMEM)
    vmem = pl.BlockSpec(memory_space=pltpu.VMEM)
    anyspec = pl.BlockSpec(memory_space=pl.ANY)
    dma = pltpu.SemaphoreType.DMA
    return pl.pallas_call(
        functools.partial(lift_conv_kernel, views, bricks),
        out_shape=jax.ShapeDtypeStruct((size_x, size_y, ch, depth), jnp.bfloat16),
        in_specs=[smem, smem, smem, vmem, anyspec, vmem, vmem, vmem],
        out_specs=anyspec,
        scratch_shapes=[
            pltpu.VMEM((min(slots, RING), pixels, voxels), jnp.bfloat16),
            pltpu.VMEM((parts, slots, ch, depth), jnp.bfloat16),
            pltpu.VMEM((parts, slots, ch, depth), jnp.bfloat16),
            pltpu.VMEM((slots + 1, ch, depth), jnp.float32),
            pltpu.VMEM((slots, 8, 128), jnp.int32),
            pltpu.VMEM((slots, 8, 128), jnp.int32),
            pltpu.VMEM((2, 8, 128), jnp.int32),
            pltpu.SMEM((2, 8, 128), jnp.int32),
            pltpu.VMEM((parts, size_x + 4, across + 1, ch, depth), jnp.bfloat16),
            pltpu.VMEM((size_x + 2, parts, across + 1, ch, depth), jnp.float32),
            pltpu.VMEM((2, 3 * ch, GROUP * depth), jnp.float32),
            pltpu.VMEM((size_x, size_y, ch, depth), jnp.bfloat16),
            pltpu.VMEM((3, 3 * ch, 6 * ch), jnp.bfloat16),
            pltpu.VMEM((3, 3 * ch, 3 * ch), jnp.bfloat16),
            pltpu.VMEM((ch, depth), jnp.float32),
            dma((min(slots, RING),)),
            dma((parts,)),
            dma((parts,)),
            dma,
            dma,
            dma,
            dma((parts, 5)),
            dma((parts, 5)),
            dma((size_x,)),
        ],
        compiler_params=pltpu.CompilerParams(
            collective_id=0, has_side_effects=True, vmem_limit_bytes=LIMIT
        ),
        name="lift_conv",
    )(pixel, voxel, count, feats, tiles, weight, bias, coef)


def turn_kernel(in_ref, out_ref, stage):
    size_y, ch, depth = in_ref.shape[1:]
    for y in range(size_y):
        stage[pl.ds(y, ch, stride=size_y), :] = in_ref[0, y].astype(jnp.float32)
    out_ref[...] = stage[...].reshape(ch, 1, size_y, depth).astype(jnp.bfloat16)


def turn(x):
    size_x, size_y, ch, depth = x.shape
    return pl.pallas_call(
        turn_kernel,
        out_shape=jax.ShapeDtypeStruct((ch, size_x, size_y, depth), jnp.bfloat16),
        grid=(size_x,),
        in_specs=[pl.BlockSpec((1, size_y, ch, depth), lambda i: (i, 0, 0, 0))],
        out_specs=pl.BlockSpec((ch, 1, size_y, depth), lambda i: (0, i, 0, 0)),
        scratch_shapes=[pltpu.VMEM((ch * size_y, depth), jnp.float32)],
        name="turn",
    )(x)


def on_device(
    views, bricks,
    tile_pixel, tile_voxel, tile_count, features, interp, conv_weight, conv_bias, smooth_coef
):
    out = lift_conv(
        tile_pixel, tile_voxel, tile_count, features[0, 0], interp[0, 0],
        conv_weight, conv_bias[None], smooth_coef, views, bricks,
    )
    return turn(out)


def solution(mesh):
    in_specs = (
        P("views", "bricks", None),
        P("views", "bricks", None),
        P("views", "bricks"),
        P("views", "bricks", None, None, None),
        P("views", "bricks", None, None, None),
        P(),
        P(),
        P("bricks", "views", None),
    )
    out_specs = P(None, "bricks", "views", None)
    body = functools.partial(on_device, mesh.shape["views"], mesh.shape["bricks"])
    return jax.shard_map(body, mesh=mesh, in_specs=in_specs, out_specs=out_specs, check_vma=False)
```

```python
import functools

import jax
import jax.numpy as jnp
from jax import lax
from jax.experimental import pallas as pl
from jax.experimental.pallas import tpu as pltpu
from jax.sharding import PartitionSpec as P

MESH = pl.DeviceIdType.MESH
GROUP = 4
RING = 32
LIMIT = 60 * 1024 * 1024
PAIRS = ((0, 1), (1, 2), (0, 2))


def lift_conv_kernel(
    views, bricks, pixel_ref, voxel_ref, count_ref, feats_ref, tiles_ref, w_ref, bias_ref,
    coef_ref, out_ref,
    tiles, part, got, sums, mark, marks, table, index, pad, acc, prod, obuf, pair, one, full, shift,
    tile_sem, send_sem, recv_sem, mark_send, mark_recv, table_sem, halo_send, halo_recv, out_sem,
):
    v = lax.axis_index("views")
    b = lax.axis_index("bricks")
    slots = voxel_ref.shape[2]
    ring = tiles.shape[0]
    me = v * bricks + b
    parts, _, ch, depth = part.shape
    size_x, size_y = obuf.shape[:2]
    across = size_y // parts
    blocks = size_x * across
    order = [parts - 1] + list(range(parts - 1))
    wide = 3 * ch

    def loop(low, high, body, unroll=1):
        def step(i, _):
            body(i)
            return 0

        lax.fori_loop(low, high, step, 0, unroll=unroll)

    def peer(k):
        turn = k + (views // 2) * bricks
        return lax.rem(v + turn // bricks, views), lax.rem(b + lax.rem(turn, bricks), bricks)

    def place(k):
        pv, pb = peer(k)
        return pv * bricks + pb

    own = (views - views // 2) * bricks % slots

    def fetch(k):
        slot = lax.rem(k, ring)
        return pltpu.make_async_copy(tiles_ref.at[place(k)], tiles.at[slot], tile_sem.at[slot])

    loop(0, ring, lambda k: fetch(k).start())
    barrier = pltpu.get_barrier_semaphore()

    def greet(k):
        @pl.when(k != own)
        def _():
            pl.semaphore_signal(barrier, inc=1, device_id=peer(k), device_id_type=MESH)

    loop(0, slots, greet)
    offset = lax.rem(me * 37, slots)

    def note(s):
        turn = lax.rem(s - offset + slots, slots)
        ident = jnp.where(turn < count_ref[0, 0], voxel_ref[0, 0, s], blocks)
        mark[s] = jnp.full(mark.shape[1:], ident, jnp.int32)

    loop(0, slots, note)

    def push(q, k):
        @pl.when(k != own)
        def _():
            pltpu.make_async_remote_copy(
                src_ref=part.at[q, place(k)], dst_ref=got.at[q, me],
                send_sem=send_sem.at[q], recv_sem=recv_sem.at[q],
                device_id=peer(k), device_id_type=MESH,
            ).start()

        @pl.when(k == own)
        def _():
            pltpu.make_async_copy(part.at[q, me], got.at[q, me], recv_sem.at[q]).start()

    def push_mark(k):
        @pl.when(k != own)
        def _():
            pltpu.make_async_remote_copy(
                src_ref=mark.at[place(k)], dst_ref=marks.at[me],
                send_sem=mark_send, recv_sem=mark_recv,
                device_id=peer(k), device_id_type=MESH,
            ).start()

        @pl.when(k == own)
        def _():
            pltpu.make_async_copy(mark.at[me], marks.at[me], mark_recv).start()

    def lift(k):
        slot = place(k)
        fetch(k).wait()
        value = jnp.dot(
            feats_ref[pixel_ref[0, 0, slot]], tiles[lax.rem(k, ring)],
            preferred_element_type=jnp.float32,
        ).astype(jnp.bfloat16)
        for q in range(parts):
            part[q, slot] = value[:, q * depth : (q + 1) * depth]
        if ring < slots:

            @pl.when(k + ring < slots)
            def _():
                fetch(k + ring).start()

    def lift_push(k):
        lift(k)
        push(order[0], k - 1)

    lift(0)
    pl.semaphore_wait(barrier, slots - 1)
    loop(1, slots, lift_push)
    push(order[0], slots - 1)
    loop(0, slots, push_mark)
    for q in order[1:]:
        loop(0, slots, lambda k, q=q: push(q, k))

    def there(dv, db):
        return (v + dv >= 0) & (v + dv < views) & (b + db >= 0) & (b + db < bricks)

    def low_row(q):
        return 1 if 2 * q >= parts else 0

    def edges(q):
        dv = 1 if 2 * q >= parts else -1
        return ((0, 1), (0, -1), (dv, 0), (dv, 1), (dv, -1))

    def span(q, dv, db):
        width = 2 if dv == 0 or q in (0, parts - 1) else 1
        if db == 0:
            from_x, to_x = pl.ds(2, size_x), pl.ds(2, size_x)
        elif db == 1:
            from_x, to_x = pl.ds(size_x + 2 - width, width), pl.ds(2 - width, width)
        else:
            from_x, to_x = pl.ds(2, width), pl.ds(size_x + 2, width)
        if dv == 0:
            return from_x, pl.ds(low_row(q), across), to_x, pl.ds(low_row(q), across)
        if dv == 1:
            return from_x, pl.ds(across, 1), to_x, pl.ds(0, 1)
        return from_x, pl.ds(0, 1), to_x, pl.ds(across, 1)

    def halo(q, k):
        dv, db = edges(q)[k]
        from_x, from_y, to_x, to_y = span(q, dv, db)
        return pltpu.make_async_remote_copy(
            src_ref=pad.at[q, from_x, from_y], dst_ref=pad.at[q, to_x, to_y],
            send_sem=halo_send.at[q, k], recv_sem=halo_recv.at[q, k],
            device_id=(v + dv, b + db), device_id_type=MESH,
        )

    for q in range(parts):
        for k, (dv, db) in enumerate(edges(q)):

            @pl.when(jnp.logical_not(there(-dv, -db)))
            def _(q=q, dv=dv, db=db):
                _, _, to_x, to_y = span(q, dv, db)
                view = pad.at[q, to_x, to_y]
                view[...] = jnp.zeros(view.shape, jnp.bfloat16)

    for dy in range(3):
        one[dy] = jnp.concatenate(
            [
                jnp.concatenate([w_ref[dx, dy, dz] for dz in range(3)], axis=0)
                for dx in range(3)
            ],
            axis=1,
        )
    for i, (first, second) in enumerate(PAIRS):
        pair[i] = jnp.concatenate([one[first], one[second]], axis=1)
    full[...] = jnp.concatenate([one[dy] for dy in range(3)], axis=1)
    tall = lax.broadcasted_iota(jnp.int32, (ch, ch), 0)
    flat = lax.broadcasted_iota(jnp.int32, (ch, ch), 1)
    spread = jnp.where(tall == flat, jnp.broadcast_to(bias_ref[...], (ch, ch)), 0.0)
    shift[...] = jnp.broadcast_to(jnp.sum(spread, axis=1, keepdims=True), shift.shape)

    pltpu.make_async_copy(marks, marks, mark_recv).wait()
    lane = lax.broadcasted_iota(jnp.int32, marks.shape[1:], 1)
    row = jnp.full(lane.shape, -1, jnp.int32)
    row = lax.fori_loop(0, slots, lambda d, r: jnp.where(lane == d, marks[d], r), row)

    def newest(match):
        found = jnp.max(jnp.where(match, lane, -1), axis=1, keepdims=True)
        return jnp.where(found < 0, slots, found)

    table[0] = lax.fori_loop(
        0, slots,
        lambda d, t: jnp.where(lane == d, newest((row == marks[d]) & (lane < d)), t),
        jnp.zeros(lane.shape, jnp.int32),
    )
    table[1] = lax.fori_loop(
        0, blocks,
        lambda i, t: jnp.where(lane == i, newest(row == i), t),
        jnp.zeros(lane.shape, jnp.int32),
    )
    to_scalar = pltpu.make_async_copy(table, index, table_sem)
    to_scalar.start()
    to_scalar.wait()
    sums[slots] = jnp.zeros(sums.shape[1:], jnp.float32)

    def receive(q):
        pltpu.make_async_copy(got.at[q], got.at[q], recv_sem.at[q]).wait()

        def add(d):
            sums[d] = sums[index[0, 0, d]] + got[q, d].astype(jnp.float32)

        def put(i):
            i = lax.rem(i + (size_x - 2) * across, blocks)
            value = jnp.maximum(sums[index[1, 0, i]], 0.0).astype(jnp.bfloat16)
            pad[q, 2 + i // across, lax.rem(i, across) + low_row(q)] = value

        loop(0, slots, add, 4)
        loop(0, blocks, put, 4)
        for k, (dv, db) in enumerate(edges(q)):

            @pl.when(there(dv, db))
            def _(k=k):
                halo(q, k).start()

    def halos(q):
        for k, (dv, db) in enumerate(edges(q)):

            @pl.when(there(-dv, -db))
            def _(k=k):
                halo(q, k).wait_recv()

    wave = lax.broadcasted_iota(jnp.int32, (ch, depth), 1)

    def beside_z(low, high):
        before = jnp.where(wave == 0, 0.0, pltpu.roll(low, 1, 1))
        after = jnp.where(wave == depth - 1, 0.0, pltpu.roll(high, depth - 1, 1))
        return before + after

    def start(slot, job):
        items, q, sources, weight, first, final = job
        n = len(items) * depth
        tall = [
            jnp.concatenate([pad[p, g + dx, y + dy] for g, y in items], axis=1)
            for p, dy in sources
            for dx in range(3)
        ]
        prod[slot, :, 0:n] = jnp.dot(
            weight[...], jnp.concatenate(tall, axis=0), preferred_element_type=jnp.float32
        )

    def finish(slot, job, keep=None):
        items, q, sources, weight, first, final = job
        for j, (g, y) in enumerate(items):
            at = slice(j * depth, (j + 1) * depth)
            value = prod[slot, ch : 2 * ch, at]
            value = value + beside_z(prod[slot, 0:ch, at], prod[slot, 2 * ch : wide, at])
            if not first:
                value = value + acc[g, q, y]
            if final:
                value = jnp.maximum(value + shift[...], 0.0)
                if keep is not None:
                    value = value * keep
            acc[g, q, y] = value

    def place_of(y):
        q = y % parts
        return q, y // parts + low_row(q)

    def smooth(x, y):
        here = acc[(x + 1,) + place_of(y)]
        beside = acc[(x,) + place_of(y)] + acc[(x + 2,) + place_of(y)]
        beside = beside + acc[(x + 1,) + place_of(y - 1)] + acc[(x + 1,) + place_of(y + 1)]
        beside = beside + beside_z(here, here)
        coef = coef_ref[x, y : y + 1, :]
        obuf[x, y] = (here + coef * (beside - 6.0 * here)).astype(jnp.bfloat16)

    def put_out(x):
        pltpu.make_async_copy(obuf.at[x], out_ref.at[x], out_sem.at[x]).start()

    def run(jobs, x=None, rows=(), keep=None):
        each = -(-len(rows) // len(jobs))
        for i, job in enumerate(jobs):
            start(i % 2, job)
            for y in rows[i * each : (i + 1) * each]:
                smooth(x, y)
            if i:
                finish((i - 1) % 2, jobs[i - 1], keep)
        finish((len(jobs) - 1) % 2, jobs[-1], keep)

    def plane(g, q, sources, weight, first, final):
        low = 0 if q == 1 else 1
        high = across + 1 if q == 2 else across
        ys = list(range(low, high))
        return [
            ([(g, y) for y in ys[i : i + GROUP]], q, sources, weight, first, final)
            for i in range(0, len(ys), GROUP)
        ]

    def line(y, q, gs):
        before, after = (q - 1) % parts, (q + 1) % parts
        sources = ((before, 0), (q, 0), (after, 0))
        return [
            ([(g, y) for g in gs[i : i + GROUP]], q, sources, full, True, True)
            for i in range(0, len(gs), GROUP)
        ]

    last = parts - 1
    both = ((last, 0), (0, 0))

    def wipe(gs, qs, ys):
        for g in gs:
            for q in qs:
                for y in ys:
                    acc[g, q, y] = jnp.zeros((ch, depth), jnp.float32)

    def first_pass(g):
        run(
            plane(g, 0, both, pair.at[0], True, False)
            + plane(g, last, both, pair.at[1], True, False)
        )

    def second_pass(g):
        run(
            plane(g, 0, ((1, 0),), one.at[2], False, True)
            + plane(g, 1, ((0, 0), (1, 0)), pair.at[0], True, False)
            + plane(g, 2, ((1, -1), (last, 0)), pair.at[2], True, False)
        )

    def outer(i):
        return jnp.where(i < 2, i, size_x - 2 + i)

    receive(order[0])
    receive(order[1])
    loop(2, size_x, first_pass)
    receive(order[2])
    loop(2, size_x, second_pass)
    receive(order[3])

    def close(g):
        return (
            plane(g, 1, ((2, 1),), one.at[2], False, True)
            + plane(g, 2, ((2, 0),), one.at[1], False, True)
            + plane(g, last, ((2, 0),), one.at[0], False, True)
        )

    inner = list(range(2, size_y - 2))
    whole = list(range(size_y))
    loop(2, 5, lambda g: run(close(g)))
    loop(5, size_x, lambda g: run(close(g), g - 3, inner))
    halos(order[0])
    halos(order[1])
    loop(0, 4, lambda i: first_pass(outer(i)))
    halos(order[2])
    loop(0, 4, lambda i: second_pass(outer(i)))
    halos(order[3])
    near, far = list(range(1, size_x + 1)), list(range(size_x + 2))
    run(line(0, last, near) + line(across, 0, near) + line(0, 0, far) + line(across, last, far))

    @pl.when(v == 0)
    def _():
        wipe(near, (last,), (0,))

    @pl.when(v == views - 1)
    def _():
        wipe(near, (0,), (across,))

    for g, edge in ((0, b == 0), (size_x + 1, b == bricks - 1)):

        @pl.when(edge)
        def _(g=g):
            wipe((g,), (0,), range(across))
            wipe((g,), (last,), (across,))

    def early(x):
        for y in (0, 1, size_y - 2, size_y - 1):
            smooth(x, y)
        put_out(x)

    loop(2, size_x - 3, early)

    def rest(i):
        low = lax.rem(i, 2) == 0
        g = jnp.where(low, 1 - i // 2, size_x + i // 2)
        x = jnp.where(
            i == 0, size_x - 3, jnp.where(i == 1, 1, jnp.where(i == 2, size_x - 2, 0))
        )
        fits = jnp.where(i < 2, 0, jnp.where(low, b, bricks - 1 - b) - 1) >= 0
        run(close(g), x, whole, jnp.where(fits, 1.0, 0.0))
        put_out(x)

    loop(0, 4, rest)

    def ending(i):
        for j in range(parts):
            smooth_last(i, j)

    def smooth_last(k, q):
        x = size_x - 1
        base = k + low_row(q)

        def spot(p):
            if p < 0:
                return parts - 1, k + low_row(parts - 1) - 1
            if p >= parts:
                return 0, k + 1 + low_row(0)
            return p, k + low_row(p)

        here = acc[x + 1, q, base]
        beside = acc[x, q, base] + acc[x + 2, q, base]
        beside = beside + acc[(x + 1,) + spot(q - 1)] + acc[(x + 1,) + spot(q + 1)]
        beside = beside + beside_z(here, here)
        coef = coef_ref[x, pl.ds(k * parts + q, 1), :]
        value = here + coef * (beside - 6.0 * here)
        obuf[x, k * parts + q] = value.astype(jnp.bfloat16)

    loop(0, across, ending)
    put_out(size_x - 1)
    for x in range(size_x):
        pltpu.make_async_copy(obuf.at[x], out_ref.at[x], out_sem.at[x]).wait()
    for q in range(parts):
        sent = part.at[q, pl.ds(0, slots - 1)]
        pltpu.make_async_copy(sent, sent, send_sem.at[q]).wait()
        for k, (dv, db) in enumerate(edges(q)):

            @pl.when(there(dv, db))
            def _(q=q, k=k):
                halo(q, k).wait_send()

    sent = mark.at[pl.ds(0, slots - 1)]
    pltpu.make_async_copy(sent, sent, mark_send).wait()


def lift_conv(pixel, voxel, count, feats, tiles, weight, bias, coef, views, bricks):
    slots, pixels, voxels = tiles.shape
    ch = feats.shape[1]
    size_x, size_y, depth = coef.shape
    parts = voxels // depth
    across = size_y // parts
    assert parts == 4
    smem = pl.BlockSpec(memory_space=pltpu.SMEM)
    vmem = pl.BlockSpec(memory_space=pltpu.VMEM)
    anyspec = pl.BlockSpec(memory_space=pl.ANY)
    dma = pltpu.SemaphoreType.DMA
    return pl.pallas_call(
        functools.partial(lift_conv_kernel, views, bricks),
        out_shape=jax.ShapeDtypeStruct((size_x, size_y, ch, depth), jnp.bfloat16),
        in_specs=[smem, smem, smem, vmem, anyspec, vmem, vmem, vmem],
        out_specs=anyspec,
        scratch_shapes=[
            pltpu.VMEM((min(slots, RING), pixels, voxels), jnp.bfloat16),
            pltpu.VMEM((parts, slots, ch, depth), jnp.bfloat16),
            pltpu.VMEM((parts, slots, ch, depth), jnp.bfloat16),
            pltpu.VMEM((slots + 1, ch, depth), jnp.float32),
            pltpu.VMEM((slots, 8, 128), jnp.int32),
            pltpu.VMEM((slots, 8, 128), jnp.int32),
            pltpu.VMEM((2, 8, 128), jnp.int32),
            pltpu.SMEM((2, 8, 128), jnp.int32),
            pltpu.VMEM((parts, size_x + 4, across + 1, ch, depth), jnp.bfloat16),
            pltpu.VMEM((size_x + 2, parts, across + 1, ch, depth), jnp.float32),
            pltpu.VMEM((2, 3 * ch, GROUP * depth), jnp.float32),
            pltpu.VMEM((size_x, size_y, ch, depth), jnp.bfloat16),
            pltpu.VMEM((3, 3 * ch, 6 * ch), jnp.bfloat16),
            pltpu.VMEM((3, 3 * ch, 3 * ch), jnp.bfloat16),
            pltpu.VMEM((3 * ch, 9 * ch), jnp.bfloat16),
            pltpu.VMEM((ch, depth), jnp.float32),
            dma((min(slots, RING),)),
            dma((parts,)),
            dma((parts,)),
            dma,
            dma,
            dma,
            dma((parts, 5)),
            dma((parts, 5)),
            dma((size_x,)),
        ],
        compiler_params=pltpu.CompilerParams(
            collective_id=0, has_side_effects=True, vmem_limit_bytes=LIMIT
        ),
        name="lift_conv",
    )(pixel, voxel, count, feats, tiles, weight, bias, coef)


def on_device(
    views, bricks,
    tile_pixel, tile_voxel, tile_count, features, interp, conv_weight, conv_bias, smooth_coef
):
    out = lift_conv(
        tile_pixel, tile_voxel, tile_count, features[0, 0], interp[0, 0],
        conv_weight, conv_bias[None], smooth_coef, views, bricks,
    )
    return jnp.transpose(out, (2, 0, 1, 3))


def solution(mesh):
    in_specs = (
        P("views", "bricks", None),
        P("views", "bricks", None),
        P("views", "bricks"),
        P("views", "bricks", None, None, None),
        P("views", "bricks", None, None, None),
        P(),
        P(),
        P("bricks", "views", None),
    )
    out_specs = P(None, "bricks", "views", None)
    body = functools.partial(on_device, mesh.shape["views"], mesh.shape["bricks"])
    return jax.shard_map(body, mesh=mesh, in_specs=in_specs, out_specs=out_specs, check_vma=False)
```
